512 devices in a mesh: row: 16 (over y, x), col: 16 (over z), depth: 2 (over core).
Axes of the slice: x: 4, y: 4, z: 16, core: 2. Of those that a mesh axis runs over, the one named last changes fastest.
Arguments:
- left_store: float32 [16, 2, 16, 2, 64, 1024], P('row', 'depth', 'col'), may hold values from -6 to 6
- left_home: int32 [16, 2, 16], P('row', 'depth'), may hold values from 0 to 15, each once within a row
- up_store: float32 [16, 2, 16, 2, 64, 1024], P('col', 'depth', 'row'), may hold values from -0.3125 to 0.3125
- up_home: int32 [16, 2, 16], P('col', 'depth'), may hold values from 0 to 15, each once within a row
- targets: int32 [16, 16, 2], P('row', 'col'), may hold values from 0 to 63, as said below
- sketch: float32 [16, 16, 2, 64, 1024], P('row', 'col'), may hold values from -0.1875 to 0.1875
Outputs:
- basis: float32 [16, 16, 2, 64, 1024], P('row', 'col', 'depth')
- weights: float32 [16, 16, 2, 64, 1024], P('row', 'col', 'depth')
The draws below stay inside these ranges and needn't reach their ends.
Inputs may be any that keep to these rules, and one draw needn't show every extreme that they name: `left_home`: for each row and depth index the entries are the store positions 0 to 15, each once. `up_home`: for each col and depth index the entries are the store positions 0 to 15, each once. `targets`: the 2 entries of one row and col index are distinct.
All inputs are finite; a program needn't handle non-finite values.
Results may differ from the reference program's by a relative error of at most 0.0003.
Values sent between devices are 32-bit elements; how exact they have to be, the bound alone decides.
No kernel may reach another device: no remote copies, remote signals or barrier semaphores. Data moves between devices by JAX's collectives and lax.ppermute only.
A program may use at most 128 MiB of HBM per device.

```python
import jax
import jax.numpy as jnp
from jax import lax

TILE = 1024
R = 64
KD = 2
RB = 8
CB = 8
TPD = 2
N_ROW = 16
N_COL = 16
N_DEPTH = 2


def draw_targets(key, part):
    keys = jax.random.split(jax.random.fold_in(key, 17), N_ROW * N_COL)
    orders = jax.vmap(lambda single: jax.random.permutation(single, RB * CB))(keys)
    return orders[:, :TPD].reshape(N_ROW, N_COL, TPD).astype(jnp.int32)


def block_scale(own_key, dims, cuts, least, top_value):
    loudness = 1.0
    for dim, blocks in cuts:
        heights = jax.random.uniform(jax.random.fold_in(jax.random.fold_in(own_key, 6), dim), (blocks,), jnp.float32, least / len(cuts), top_value / len(cuts))
        loudness = loudness * jnp.repeat(jnp.exp(heights), dims[dim] // blocks).reshape((-1,) + (1,) * (len(dims) - 1 - dim))
    return loudness


def gaussian(rng, extent, deviation, reach, cuts=(), kind=jnp.bfloat16):
    gain = block_scale(rng, extent, cuts, -0.22, 0.18) if cuts else 1.0
    drawn = jax.random.normal(rng, extent, jnp.float32) * deviation * gain
    return jnp.minimum(jnp.maximum(drawn, -reach), reach).astype(kind)


def setup_inputs(seed: int = 0) -> dict:
    key_list = jax.random.split(jax.random.key(seed), 7)
    return {
        "left_store": gaussian(key_list[0], (N_ROW, N_DEPTH, RB * KD, 2, R, TILE), 1.0, 6.0, ((0, 16), (1, 2), (2, 16)), jnp.float32),
        "left_home": jax.vmap(lambda own: jax.random.permutation(own, RB * KD))(jax.random.split(key_list[1], N_ROW * N_DEPTH)).reshape((N_ROW, N_DEPTH, RB * KD)).astype(jnp.int32),
        "up_store": gaussian(key_list[2], (N_COL, N_DEPTH, CB * KD, 2, R, TILE), (6 * R) ** -0.5, 0.3125, ((0, 16), (1, 2), (2, 16)), jnp.float32),
        "up_home": jax.vmap(lambda own: jax.random.permutation(own, CB * KD))(jax.random.split(key_list[3], N_COL * N_DEPTH)).reshape((N_COL, N_DEPTH, CB * KD)).astype(jnp.int32),
        "targets": draw_targets(jax.random.fold_in(key_list[6], 71), 0),
        "sketch": gaussian(key_list[5], (N_ROW, N_COL, TPD, R, TILE), TILE ** -0.5, 0.1875, ((0, 16), (1, 16)), jnp.float32),
    }


def orthonormal(sample):
    gram_mat = jnp.einsum('pat,pbt->pab', sample, sample, precision=lax.Precision.HIGHEST)
    factor_low = jnp.linalg.cholesky(gram_mat)
    return lax.linalg.triangular_solve(factor_low, sample, left_side=True, lower=True)

def reference(left_store, left_home, up_store, up_home, targets, sketch):
    pick = jax.vmap(jax.vmap(lambda store, home: jnp.take(store, home, axis=0)))
    left_order = pick(left_store, left_home).reshape(N_ROW, N_DEPTH, RB, KD, 2, R, TILE)
    up_order = pick(up_store, up_home).reshape(N_COL, N_DEPTH, CB, KD, 2, R, TILE)
    high = lax.Precision.HIGHEST

    def per_cell(cell):
        row_index = cell // N_COL
        col_index = cell % N_COL
        chosen = targets[row_index, col_index]
        block_row = (chosen // CB).astype(jnp.int32)
        block_col = (chosen % CB).astype(jnp.int32)
        row_pairs = jnp.take(left_order[row_index], block_row, axis=1)
        col_pairs = jnp.take(up_order[col_index], block_col, axis=1)
        row_basis = row_pairs[:, :, :, 0]
        row_coef = row_pairs[:, :, :, 1]
        col_coef = col_pairs[:, :, :, 0]
        col_basis = col_pairs[:, :, :, 1]
        test_rows = sketch[row_index, col_index]
        middle = jnp.einsum('dpkat,dpkbt->dpkab', row_coef, col_coef, precision=high)
        test_side = jnp.einsum('pat,dpkbt->dpkab', test_rows, col_basis, precision=high)
        folded = jnp.einsum('dpkab,dpkcb->dpkac', test_side, middle, precision=high)
        sampled = jnp.einsum('dpkac,dpkct->pat', folded, row_basis, precision=high)
        bases = orthonormal(sampled)
        inner_prod = jnp.einsum('pat,dpkct->dpkac', bases, row_basis, precision=high)
        turned = jnp.einsum('dpkac,dpkcb->dpkab', inner_prod, middle, precision=high)
        projected = jnp.einsum('dpkab,dpkbt->pat', turned, col_basis, precision=high)
        root_tile = jnp.sqrt(jnp.float32(TILE))
        return (bases * root_tile, projected / root_tile)
    basis, weights = lax.map(per_cell, jnp.arange(N_ROW * N_COL, dtype=jnp.int32))
    return (basis.reshape(N_ROW, N_COL, TPD, R, TILE), weights.reshape(N_ROW, N_COL, TPD, R, TILE))
```

```python
import math

import jax
import jax.numpy as jnp
from jax import lax
from jax.experimental import pallas as pl
from jax.experimental.pallas import tpu as pltpu
from jax.sharding import PartitionSpec as P


KD = 2
CB = 8
SIDE = 4
HIGH = lax.Precision.HIGHEST
UP_AT, TARGET_AT, ROW_AT, COL_AT, DEPTH_AT = 16, 32, 34, 35, 36


def z_shift(n_col):
    return [(c * 2 + d, ((c + (1 - 2 * d)) % n_col) * 2 + d) for c in range(n_col) for d in (0, 1)]


def xy_shift(step, phase):
    pairs = []
    for r in range(SIDE * SIDE):
        y, x = divmod(r, SIDE)
        for d in (0, 1):
            if (d + phase) % 2 == 0:
                to = y * SIDE + (x + step) % SIDE
            else:
                to = (y + step) % SIDE * SIDE + x
            pairs.append((r * 2 + d, to * 2 + d))
    return pairs


SWAP = [(0, 1), (1, 0)]


def ring_steps(info, position):
    way = info[COL_AT] - position
    return jnp.where(info[DEPTH_AT] == 0, way, -way) & 15


def up_place(info, position):
    row = info[ROW_AT]
    dy = (row // SIDE - position // SIDE) & (SIDE - 1)
    dx = (row - position) & (SIDE - 1)
    first = info[DEPTH_AT] == 0
    return jnp.where(first, dy, dx), jnp.where(first, dx, dy)


def up_choice_kernel(info, u0, u1, u2, u3, out, sems):
    ups = (u0, u1, u2, u3)
    tile = info[TARGET_AT + 1 - info[DEPTH_AT]]
    j = tile % CB
    for k in range(KD):
        t, s = up_place(info, info[UP_AT + j * KD + k])
        for i in range(SIDE):

            @pl.when(t == i)
            def _():
                pltpu.make_async_copy(ups[i].at[s], out.at[k], sems.at[k]).start()

    for k in range(KD):
        pltpu.make_async_copy(u0.at[0], out.at[k], sems.at[k]).wait()


def left_choice_kernel(info, other, *refs):
    own, across, out, sems = refs[:7], refs[7:14], refs[14], refs[15]
    tile = info[TARGET_AT + 1 - info[DEPTH_AT]]
    b = tile // CB
    for kind, (table, pieces) in enumerate(((info, own), (other, across))):
        for k in range(KD):
            slot = (1 - kind) * KD + k
            s = ring_steps(info, table[b * KD + k])
            for i in range(7):

                @pl.when(s == i + 1)
                def _():
                    pltpu.make_async_copy(pieces[i], out.at[slot], sems.at[slot]).start()

            @pl.when((s >= 1) & (s <= 7))
            def _():
                pltpu.make_async_copy(pieces[0], out.at[slot], sems.at[slot]).wait()


def dot(a, b, contract):
    return lax.dot_general(a, b, ((contract[:1], contract[1:]), ((), ())), precision=HIGH, preferred_element_type=jnp.float32)


def inverse_factor(gram):
    n = gram.shape[0]
    row_id = lax.broadcasted_iota(jnp.int32, (n, n), 0)
    lane_id = lax.broadcasted_iota(jnp.int32, (n, n), 1)
    eye = jnp.where(row_id == lane_id, jnp.float32(1), jnp.float32(0))
    work = jnp.concatenate([gram, eye], axis=1)
    blocks = [work[8 * i : 8 * i + 8] for i in range(n // 8)]
    sub = lax.broadcasted_iota(jnp.int32, (8, 2 * n), 0)
    for k in range(n):
        at, within = divmod(k, 8)
        row = blocks[at][within : within + 1]
        scale = lax.rsqrt(row[:, k : k + 1])
        row = row * scale
        for i in range(at, n // 8):
            change = (blocks[i][:, k : k + 1] * scale) * row
            if i == at:
                blocks[i] = jnp.where(sub > within, blocks[i] - change, jnp.where(sub == within, row, blocks[i]))
            else:
                blocks[i] = blocks[i] - change
    return jnp.concatenate(blocks, axis=0)[:, n:]


def tile_kernel(info, other, *refs):
    own, across = refs[:9], refs[9:17]
    left_in, last_in = refs[17:19]
    ups, up_in, sketch = refs[19:23], refs[23], refs[24]
    basis_out, weights_out = refs[25:27]
    xs, ys, ps, qs, ws, left_sems, up_sems, sketch_sem = refs[27:]
    depth = info[DEPTH_AT]
    tile = info[TARGET_AT + depth]
    b, j = tile // CB, tile % CB
    n, size = ws.shape

    def left_copies(source, slot):
        return (
            pltpu.make_async_copy(source.at[0], xs.at[slot], left_sems.at[slot, 0]),
            pltpu.make_async_copy(source.at[1], ys.at[slot], left_sems.at[slot, 1]),
        )

    def up_copies(source, slot):
        return (
            pltpu.make_async_copy(source.at[0], ps.at[slot], up_sems.at[slot, 0]),
            pltpu.make_async_copy(source.at[1], qs.at[slot], up_sems.at[slot, 1]),
        )

    def start(condition, copies):
        @pl.when(condition)
        def _():
            for copy in copies:
                copy.start()

    pltpu.make_async_copy(sketch.at[depth], ws, sketch_sem).start()
    for kind, (table, pieces) in enumerate(((info, own), (other, across))):
        for k in range(KD):
            slot = kind * KD + k
            s = ring_steps(info, table[b * KD + k])
            for i, piece in enumerate(pieces):
                start(s == i, left_copies(piece, slot))
            if kind == 1:
                start(s == 8, left_copies(last_in, slot))
            start(s > 8, left_copies(left_in.at[slot], slot))
            if kind == 0:
                t, s = up_place(info, table[UP_AT + j * KD + k])
                for i in range(SIDE):
                    start(t == i, up_copies(ups[i].at[s], slot))
            else:
                for copy in up_copies(up_in.at[k], slot):
                    copy.start()
    pltpu.make_async_copy(sketch.at[0], ws, sketch_sem).wait()
    slots = 2 * KD
    for slot in range(slots):
        for copy in (*up_copies(up_in.at[0], slot), *left_copies(own[0], slot)):
            copy.wait()
    x_all = xs[...].reshape(slots * n, size)
    q_all = qs[...].reshape(slots * n, size)
    tested = dot(ws[...], q_all, (1, 1))
    middles = [dot(ys[i], ps[i], (1, 1)) for i in range(slots)]
    folded = jnp.concatenate([dot(tested[:, i * n : i * n + n], middles[i], (1, 1)) for i in range(slots)], axis=1)
    sample = dot(folded, x_all, (1, 0))
    inverse = inverse_factor(dot(sample, sample, (1, 1)))
    bases = dot(inverse, sample, (1, 0))
    root = math.sqrt(size)
    basis_out[...] = bases * root
    inner = dot(bases, x_all, (1, 1))
    turned = jnp.concatenate([dot(inner[:, i * n : i * n + n], middles[i], (1, 0)) for i in range(slots)], axis=1)
    weights_out[...] = dot(turned, q_all, (1, 0)) * (1 / root)


def local_kernel(kernel, n_scalar, n_any, out_shape, out_space, scratch, mebibytes=1):
    return pl.pallas_call(
        kernel,
        out_shape=out_shape,
        in_specs=[pl.BlockSpec(memory_space=pltpu.SMEM)] * n_scalar + [pl.BlockSpec(memory_space=pltpu.HBM)] * n_any,
        out_specs=jax.tree.map(lambda _: pl.BlockSpec(memory_space=out_space), out_shape),
        scratch_shapes=scratch,
        compiler_params=pltpu.CompilerParams(vmem_limit_bytes=mebibytes << 20),
    )


def pieces_and_tile(left_store, left_home, up_store, up_home, targets, sketch):
    n_col = lax.axis_size("col")
    own, up, test = left_store[0, 0, 0], up_store[0, 0, 0], sketch[0, 0]
    pair = own.shape
    places = jnp.stack([lax.axis_index(a).astype(jnp.int32) for a in ("row", "col", "depth")])
    info = jnp.concatenate([left_home[0, 0], up_home[0, 0], targets[0, 0], places])
    across = lax.ppermute(own, "depth", SWAP)
    own_pieces, across_pieces = [own], [across]
    shift = z_shift(n_col)
    half = n_col // 2
    for step in range(1, half + 1):
        own_pieces.append(lax.ppermute(own_pieces[-1], ("col", "depth"), shift))
        if step < half:
            across_pieces.append(lax.ppermute(across_pieces[-1], ("col", "depth"), shift))
    block = jnp.stack([up] + [lax.ppermute(up, ("row", "depth"), xy_shift(s, 0)) for s in range(1, SIDE)])
    ups = [block] + [lax.ppermute(block, ("row", "depth"), xy_shift(s, 1)) for s in range(1, SIDE)]
    other = lax.ppermute(info, "depth", SWAP)

    f32 = jnp.float32
    up_choice = local_kernel(up_choice_kernel, 1, SIDE, jax.ShapeDtypeStruct((KD, *pair), f32), pltpu.HBM, [pltpu.SemaphoreType.DMA((KD,))])
    up_in = lax.ppermute(up_choice(info, *ups), "depth", SWAP)
    left_choice = local_kernel(left_choice_kernel, 2, 14, jax.ShapeDtypeStruct((2 * KD, *pair), f32), pltpu.HBM, [pltpu.SemaphoreType.DMA((2 * KD,))])
    left_in = lax.ppermute(left_choice(info, other, *own_pieces[1:8], *across_pieces[1:8]), "depth", SWAP)
    last_in = lax.ppermute(own_pieces[8], "depth", SWAP)

    flat = pair[1:]
    tile = jax.ShapeDtypeStruct(flat, f32)
    stack = pltpu.VMEM((2 * KD, *flat), f32)
    sems = pltpu.SemaphoreType.DMA((2 * KD, 2))
    whole = local_kernel(tile_kernel, 2, 25, (tile, tile), pltpu.VMEM, [stack] * 4 + [pltpu.VMEM(flat, f32), sems, sems, pltpu.SemaphoreType.DMA], 12)
    basis, weights = whole(info, other, *own_pieces, *across_pieces, left_in, last_in, *ups, up_in, test)
    return basis[None, None, None], weights[None, None, None]


def solution(mesh):
    return jax.shard_map(
        pieces_and_tile,
        mesh=mesh,
        in_specs=(
            P("row", "depth", "col", None, None, None),
            P("row", "depth", None),
            P("col", "depth", "row", None, None, None),
            P("col", "depth", None),
            P("row", "col", None),
            P("row", "col", None, None, None),
        ),
        out_specs=(P("row", "col", "depth", None, None), P("row", "col", "depth", None, None)),
        check_vma=False,
    )
```

```python
import math

import jax
import jax.numpy as jnp
from jax import lax
from jax.experimental import pallas as pl
from jax.experimental.pallas import tpu as pltpu
from jax.sharding import PartitionSpec as P


KD = 2
CB = 8
SIDE = 4
HIGH = lax.Precision.HIGHEST
UP_AT, TARGET_AT, ROW_AT, COL_AT, DEPTH_AT = 16, 32, 34, 35, 36


def z_shift(n_col):
    return [(c * 2 + d, ((c + (1 - 2 * d)) % n_col) * 2 + d) for c in range(n_col) for d in (0, 1)]


def xy_shift(step, phase):
    pairs = []
    for r in range(SIDE * SIDE):
        y, x = divmod(r, SIDE)
        for d in (0, 1):
            if (d + phase) % 2 == 0:
                to = y * SIDE + (x + step) % SIDE
            else:
                to = (y + step) % SIDE * SIDE + x
            pairs.append((r * 2 + d, to * 2 + d))
    return pairs


SWAP = [(0, 1), (1, 0)]


def ring_steps(info, position):
    way = info[COL_AT] - position
    return jnp.where(info[DEPTH_AT] == 0, way, -way) & 15


def up_place(info, position):
    row = info[ROW_AT]
    dy = (row // SIDE - position // SIDE) & (SIDE - 1)
    dx = (row - position) & (SIDE - 1)
    first = info[DEPTH_AT] == 0
    return jnp.where(first, dy, dx), jnp.where(first, dx, dy)


def up_choice_kernel(info, u0, u1, u2, u3, out, sems):
    ups = (u0, u1, u2, u3)
    tile = info[TARGET_AT + 1 - info[DEPTH_AT]]
    j = tile % CB
    for k in range(KD):
        t, s = up_place(info, info[UP_AT + j * KD + k])
        for i in range(SIDE):

            @pl.when(t == i)
            def _():
                pltpu.make_async_copy(ups[i].at[s], out.at[k], sems.at[k]).start()

    for k in range(KD):
        pltpu.make_async_copy(u0.at[0], out.at[k], sems.at[k]).wait()


def left_choice_kernel(info, other, *refs):
    own, across, out, sems = refs[:7], refs[7:14], refs[14], refs[15]
    tile = info[TARGET_AT + 1 - info[DEPTH_AT]]
    b = tile // CB
    for kind, (table, pieces) in enumerate(((info, own), (other, across))):
        for k in range(KD):
            slot = (1 - kind) * KD + k
            s = ring_steps(info, table[b * KD + k])
            for i in range(7):

                @pl.when(s == i + 1)
                def _():
                    pltpu.make_async_copy(pieces[i], out.at[slot], sems.at[slot]).start()

            @pl.when((s >= 1) & (s <= 7))
            def _():
                pltpu.make_async_copy(pieces[0], out.at[slot], sems.at[slot]).wait()


def dot(a, b, contract):
    return lax.dot_general(a, b, ((contract[:1], contract[1:]), ((), ())), precision=HIGH, preferred_element_type=jnp.float32)


def inverse_factor(gram):
    n = gram.shape[0]
    row_id = lax.broadcasted_iota(jnp.int32, (n, n), 0)
    lane_id = lax.broadcasted_iota(jnp.int32, (n, n), 1)
    eye = jnp.where(row_id == lane_id, jnp.float32(1), jnp.float32(0))
    work = jnp.concatenate([gram, eye], axis=1)
    tall, wide = 8, 2 * n
    blocks = [work[tall * i : tall * i + tall] for i in range(n // tall)]
    sub = lax.broadcasted_iota(jnp.int32, (tall, wide), 0)
    spread = lambda x: jnp.broadcast_to(x, (tall, wide))
    for at in range(n // tall):
        below = n // tall - at
        columns = [[spread(blocks[at + i][:, tall * at + j : tall * at + j + 1]) for i in range(below)] for j in range(tall)]
        rows, scales, block = [], [], blocks[at]
        for w in range(tall):
            scale = lax.rsqrt(spread(columns[w][0][w : w + 1]))
            inverse = scale * scale
            row = spread(block[w : w + 1]) * inverse
            block = jnp.where(sub > w, block - columns[w][0] * row, block)
            rows.append(row)
            scales.append(scale)
            for j in range(w + 1, tall):
                part = spread(columns[j][0][w : w + 1]) * inverse
                for i in range(below):
                    new = columns[j][i] - columns[w][i] * part
                    columns[j][i] = new if i else jnp.where(sub > w, new, columns[j][i])
        scale = scales[-1]
        for w in range(tall - 1):
            scale = jnp.where(sub == w, scales[w], scale)
        blocks[at] = block * scale
        for i in range(1, below):
            for w in range(tall):
                blocks[at + i] = blocks[at + i] - columns[w][i] * rows[w]
    return jnp.concatenate(blocks, axis=0)[:, n:]


def up_kernel(info, u0, u1, u2, u3, up_in, sketch, ps, qs, tested, ws, up_sems, sketch_sem):
    ups = (u0, u1, u2, u3)
    depth = info[DEPTH_AT]
    j = info[TARGET_AT + depth] % CB
    n, size = ws.shape
    slots = 2 * KD

    def copies(source, slot):
        return (
            pltpu.make_async_copy(source.at[0], ps.at[slot], up_sems.at[slot, 0]),
            pltpu.make_async_copy(source.at[1], qs.at[slot], up_sems.at[slot, 1]),
        )

    pltpu.make_async_copy(sketch.at[depth], ws, sketch_sem).start()
    for k in range(KD):
        t, s = up_place(info, info[UP_AT + j * KD + k])
        for i in range(SIDE):

            @pl.when(t == i)
            def _():
                for copy in copies(ups[i].at[s], k):
                    copy.start()

        for copy in copies(up_in.at[k], KD + k):
            copy.start()
    pltpu.make_async_copy(sketch.at[0], ws, sketch_sem).wait()
    for slot in range(slots):
        for copy in copies(up_in.at[0], slot):
            copy.wait()
    tested[...] = dot(ws[...], qs[...].reshape(slots * n, size), (1, 1))


def tile_kernel(info, other, *refs):
    own, across = refs[:9], refs[9:17]
    left_in, last_in, ps, qs, tested = refs[17:22]
    basis_out, weights_out = refs[22:24]
    xs, ys, left_sems = refs[24:]
    b = info[TARGET_AT + info[DEPTH_AT]] // CB
    slots, n, size = xs.shape

    def copies(source, slot):
        return (
            pltpu.make_async_copy(source.at[1], ys.at[slot], left_sems.at[slot, 1]),
            pltpu.make_async_copy(source.at[0], xs.at[slot], left_sems.at[slot, 0]),
        )

    def start(condition, source, slot):
        @pl.when(condition)
        def _():
            for copy in copies(source, slot):
                copy.start()

    for kind, (table, pieces) in enumerate(((info, own), (other, across))):
        for k in range(KD):
            slot = kind * KD + k
            s = ring_steps(info, table[b * KD + k])
            for i, piece in enumerate(pieces):
                start(s == i, piece, slot)
            if kind == 1:
                start(s == 8, last_in, slot)
            start(s > 8, left_in.at[slot], slot)
    for slot in range(slots):
        for copy in copies(own[0], slot):
            copy.wait()
    x_all = xs[...].reshape(slots * n, size)
    q_all = qs[...].reshape(slots * n, size)
    middles = [dot(ys[i], ps[i], (1, 1)) for i in range(slots)]
    folded = jnp.concatenate([dot(tested[:, i * n : i * n + n], middles[i], (1, 1)) for i in range(slots)], axis=1)
    sample = dot(folded, x_all, (1, 0))
    inner = dot(sample, x_all, (1, 1))
    turned = jnp.concatenate([dot(inner[:, i * n : i * n + n], middles[i], (1, 0)) for i in range(slots)], axis=1)
    project = dot(turned, q_all, (1, 0))
    inverse = inverse_factor(dot(sample, sample, (1, 1)))
    root = math.sqrt(size)
    basis_out[...] = dot(inverse * root, sample, (1, 0))
    weights_out[...] = dot(inverse * (1 / root), project, (1, 0))


def local_kernel(kernel, in_spaces, out_shape, out_space, scratch, mebibytes=1):
    return pl.pallas_call(
        kernel,
        out_shape=out_shape,
        in_specs=[pl.BlockSpec(memory_space=space) for space in in_spaces],
        out_specs=jax.tree.map(lambda _: pl.BlockSpec(memory_space=out_space), out_shape),
        scratch_shapes=scratch,
        compiler_params=pltpu.CompilerParams(vmem_limit_bytes=mebibytes << 20),
    )


def pieces_and_tile(left_store, left_home, up_store, up_home, targets, sketch):
    n_col = lax.axis_size("col")
    own, up, test = left_store[0, 0, 0], up_store[0, 0, 0], sketch[0, 0]
    pair = own.shape
    places = jnp.stack([lax.axis_index(a).astype(jnp.int32) for a in ("row", "col", "depth")])
    info = jnp.concatenate([left_home[0, 0], up_home[0, 0], targets[0, 0], places])
    across = lax.ppermute(own, "depth", SWAP)
    own_pieces, across_pieces = [own], [across]
    shift = z_shift(n_col)
    half = n_col // 2
    for step in range(1, half + 1):
        own_pieces.append(lax.ppermute(own_pieces[-1], ("col", "depth"), shift))
        if step < half:
            across_pieces.append(lax.ppermute(across_pieces[-1], ("col", "depth"), shift))
    block = jnp.stack([up] + [lax.ppermute(up, ("row", "depth"), xy_shift(s, 0)) for s in range(1, SIDE)])
    ups = [block] + [lax.ppermute(block, ("row", "depth"), xy_shift(s, 1)) for s in range(1, SIDE)]
    other = lax.ppermute(info, "depth", SWAP)

    early = lambda pieces: [pltpu.with_memory_space_constraint(x, pltpu.HBM) for x in pieces[:7]] + pieces[7:]
    own_held, across_held = early(own_pieces), early(across_pieces)
    f32 = jnp.float32
    smem, hbm, vmem = pltpu.SMEM, pltpu.HBM, pltpu.VMEM
    slots = 2 * KD
    dma = pltpu.SemaphoreType.DMA
    choice = jax.ShapeDtypeStruct((KD, *pair), f32)
    up_choice = local_kernel(up_choice_kernel, [smem] + [hbm] * SIDE, choice, hbm, [dma((KD,))])
    up_in = lax.ppermute(up_choice(info, *ups), "depth", SWAP)
    choice = jax.ShapeDtypeStruct((slots, *pair), f32)
    left_choice = local_kernel(left_choice_kernel, [smem] * 2 + [hbm] * 14, choice, hbm, [dma((slots,))])
    left_in = lax.ppermute(left_choice(info, other, *own_held[1:8], *across_held[1:8]), "depth", SWAP)
    last_in = lax.ppermute(own_pieces[8], "depth", SWAP)

    flat = pair[1:]
    tile, stack = jax.ShapeDtypeStruct(flat, f32), jax.ShapeDtypeStruct((slots, *flat), f32)
    square = jax.ShapeDtypeStruct((flat[0], slots * flat[0]), f32)
    scratch = [vmem(flat, f32), dma((slots, 2)), dma]
    up_part = local_kernel(up_kernel, [smem] + [hbm] * (SIDE + 2), (stack, stack, square), vmem, scratch, 6)
    up_sides = up_part(info, *ups, up_in, test)
    scratch = [vmem(stack.shape, f32)] * 2 + [dma((slots, 2))]
    whole = local_kernel(tile_kernel, [smem] * 2 + [hbm] * 19 + [vmem] * 3, (tile, tile), vmem, scratch, 12)
    basis, weights = whole(info, other, *own_held, *across_held, left_in, last_in, *up_sides)
    return basis[None, None, None], weights[None, None, None]


def solution(mesh):
    return jax.shard_map(
        pieces_and_tile,
        mesh=mesh,
        in_specs=(
            P("row", "depth", "col", None, None, None),
            P("row", "depth", None),
            P("col", "depth", "row", None, None, None),
            P("col", "depth", None),
            P("row", "col", None),
            P("row", "col", None, None, None),
        ),
        out_specs=(P("row", "col", "depth", None, None), P("row", "col", "depth", None, None)),
        check_vma=False,
    )
```

```python
import math

import jax
import jax.numpy as jnp
from jax import lax
from jax.experimental import pallas as pl
from jax.experimental.pallas import tpu as pltpu
from jax.sharding import PartitionSpec as P


KD = 2
CB = 8
SIDE = 4
UP_AT, TARGET_AT, ROW_AT, COL_AT, DEPTH_AT = 16, 32, 34, 35, 36


def z_shift(n_col):
    return [(c * 2 + d, ((c + (1 - 2 * d)) % n_col) * 2 + d) for c in range(n_col) for d in (0, 1)]


def xy_shift(step, phase):
    pairs = []
    for r in range(SIDE * SIDE):
        y, x = divmod(r, SIDE)
        for d in (0, 1):
            if (d + phase) % 2 == 0:
                to = y * SIDE + (x + step) % SIDE
            else:
                to = (y + step) % SIDE * SIDE + x
            pairs.append((r * 2 + d, to * 2 + d))
    return pairs


SWAP = [(0, 1), (1, 0)]


def ring_steps(info, position):
    way = info[COL_AT] - position
    return jnp.where(info[DEPTH_AT] == 0, way, -way) & 15


def up_place(info, position):
    row = info[ROW_AT]
    dy = (row // SIDE - position // SIDE) & (SIDE - 1)
    dx = (row - position) & (SIDE - 1)
    first = info[DEPTH_AT] == 0
    return jnp.where(first, dy, dx), jnp.where(first, dx, dy)


def up_choice_kernel(info, u0, u1, u2, u3, out, sems):
    ups = (u0, u1, u2, u3)
    tile = info[TARGET_AT + 1 - info[DEPTH_AT]]
    j = tile % CB
    for k in range(KD):
        t, s = up_place(info, info[UP_AT + j * KD + k])
        for i in range(SIDE):

            @pl.when(t == i)
            def _():
                pltpu.make_async_copy(ups[i].at[s], out.at[k], sems.at[k]).start()

    for k in range(KD):
        pltpu.make_async_copy(u0.at[0], out.at[k], sems.at[k]).wait()


def left_choice_kernel(info, other, *refs):
    own, across, out, sems = refs[:7], refs[7:14], refs[14], refs[15]
    tile = info[TARGET_AT + 1 - info[DEPTH_AT]]
    b = tile // CB
    for kind, (table, pieces) in enumerate(((info, own), (other, across))):
        for k in range(KD):
            slot = (1 - kind) * KD + k
            s = ring_steps(info, table[b * KD + k])
            for i in range(7):

                @pl.when(s == i + 1)
                def _():
                    pltpu.make_async_copy(pieces[i], out.at[slot], sems.at[slot]).start()

            @pl.when((s >= 1) & (s <= 7))
            def _():
                pltpu.make_async_copy(pieces[0], out.at[slot], sems.at[slot]).wait()


def parts(x):
    high = x.astype(jnp.bfloat16)
    return high, (x - high.astype(jnp.float32)).astype(jnp.bfloat16)


def dot(a, b, contract):
    dims = ((contract[:1], contract[1:]), ((), ()))
    one = lambda u, v: lax.dot_general(u, v, dims, preferred_element_type=jnp.float32)
    (a_high, a_low), (b_high, b_low) = parts(a), parts(b)
    return one(a_high, b_high) + (one(a_high, b_low) + one(a_low, b_high))


def inverse_factor(gram):
    n = gram.shape[0]
    row_id = lax.broadcasted_iota(jnp.int32, (n, n), 0)
    lane_id = lax.broadcasted_iota(jnp.int32, (n, n), 1)
    eye = jnp.where(row_id == lane_id, jnp.float32(1), jnp.float32(0))
    work = jnp.concatenate([gram, eye], axis=1)
    tall, wide = 8, 2 * n
    blocks = [work[tall * i : tall * i + tall] for i in range(n // tall)]
    sub = lax.broadcasted_iota(jnp.int32, (tall, wide), 0)
    spread = lambda x: jnp.broadcast_to(x, (tall, wide))
    for at in range(n // tall):
        below = n // tall - at
        columns = [[spread(blocks[at + i][:, tall * at + j : tall * at + j + 1]) for i in range(below)] for j in range(tall)]
        rows, scales, block = [], [], blocks[at]
        for w in range(tall):
            scale = lax.rsqrt(spread(columns[w][0][w : w + 1]))
            inverse = scale * scale
            row = spread(block[w : w + 1]) * inverse
            block = jnp.where(sub > w, block - columns[w][0] * row, block)
            rows.append(row)
            scales.append(scale)
            for j in range(w + 1, tall):
                part = spread(columns[j][0][w : w + 1]) * inverse
                for i in range(below):
                    new = columns[j][i] - columns[w][i] * part
                    columns[j][i] = new if i else jnp.where(sub > w, new, columns[j][i])
        scale = scales[-1]
        for w in range(tall - 1):
            scale = jnp.where(sub == w, scales[w], scale)
        blocks[at] = block * scale
        for i in range(1, below):
            for w in range(tall):
                blocks[at + i] = blocks[at + i] - columns[w][i] * rows[w]
    return jnp.concatenate(blocks, axis=0)[:, n:]


def up_kernel(info, u0, u1, u2, u3, up_in, sketch, ps, qs, tested, ws, up_sems, sketch_sem):
    ups = (u0, u1, u2, u3)
    depth = info[DEPTH_AT]
    j = info[TARGET_AT + depth] % CB
    n, size = ws.shape
    slots = 2 * KD

    def copies(source, slot):
        return (
            pltpu.make_async_copy(source.at[0], ps.at[slot], up_sems.at[slot, 0]),
            pltpu.make_async_copy(source.at[1], qs.at[slot], up_sems.at[slot, 1]),
        )

    pltpu.make_async_copy(sketch.at[depth], ws, sketch_sem).start()
    for k in range(KD):
        t, s = up_place(info, info[UP_AT + j * KD + k])
        for i in range(SIDE):

            @pl.when(t == i)
            def _():
                for copy in copies(ups[i].at[s], k):
                    copy.start()

        for copy in copies(up_in.at[k], KD + k):
            copy.start()
    pltpu.make_async_copy(sketch.at[0], ws, sketch_sem).wait()
    for slot in range(slots):
        for copy in copies(up_in.at[0], slot):
            copy.wait()
    tested[...] = dot(ws[...], qs[...].reshape(slots * n, size), (1, 1))


def tile_kernel(info, other, *refs):
    own, across = refs[:9], refs[9:17]
    left_in, last_in, ps, qs, tested = refs[17:22]
    basis_out, weights_out = refs[22:24]
    xs, ys, left_sems = refs[24:]
    b = info[TARGET_AT + info[DEPTH_AT]] // CB
    slots, n, size = xs.shape

    def copies(source, slot):
        return (
            pltpu.make_async_copy(source.at[1], ys.at[slot], left_sems.at[slot, 1]),
            pltpu.make_async_copy(source.at[0], xs.at[slot], left_sems.at[slot, 0]),
        )

    def start(condition, source, slot):
        @pl.when(condition)
        def _():
            for copy in copies(source, slot):
                copy.start()

    for kind, (table, pieces) in enumerate(((info, own), (other, across))):
        for k in range(KD):
            slot = kind * KD + k
            s = ring_steps(info, table[b * KD + k])
            for i, piece in enumerate(pieces):
                start(s == i, piece, slot)
            if kind == 1:
                start(s == 8, last_in, slot)
            start(s > 8, left_in.at[slot], slot)
    for slot in range(slots):
        for copy in copies(own[0], slot):
            copy.wait()
    middles = [dot(ys[i], ps[i], (1, 1)) for i in range(slots)]
    folded = [dot(tested[:, i * n : i * n + n], middles[i], (1, 1)) for i in range(slots)]
    sample = dot(jnp.concatenate(folded, axis=1), xs[...].reshape(slots * n, size), (1, 0))
    inverse = inverse_factor(dot(sample, sample, (1, 1)))
    turned = jnp.concatenate([dot(dot(sample, xs[i], (1, 1)), middles[i], (1, 0)) for i in range(slots)], axis=1)
    root = math.sqrt(size)
    basis_out[...] = dot(inverse * root, sample, (1, 0))
    wide = size // 4
    for at in range(0, size, wide):
        project = dot(turned, qs[:, :, at : at + wide].reshape(slots * n, wide), (1, 0))
        weights_out[:, at : at + wide] = dot(inverse * (1 / root), project, (1, 0))


def local_kernel(kernel, in_spaces, out_shape, out_space, scratch, mebibytes=1):
    return pl.pallas_call(
        kernel,
        out_shape=out_shape,
        in_specs=[pl.BlockSpec(memory_space=space) for space in in_spaces],
        out_specs=jax.tree.map(lambda _: pl.BlockSpec(memory_space=out_space), out_shape),
        scratch_shapes=scratch,
        compiler_params=pltpu.CompilerParams(vmem_limit_bytes=mebibytes << 20),
    )


def pieces_and_tile(left_store, left_home, up_store, up_home, targets, sketch):
    n_col = lax.axis_size("col")
    own, up, test = left_store[0, 0, 0], up_store[0, 0, 0], sketch[0, 0]
    pair = own.shape
    places = jnp.stack([lax.axis_index(a).astype(jnp.int32) for a in ("row", "col", "depth")])
    info = jnp.concatenate([left_home[0, 0], up_home[0, 0], targets[0, 0], places])
    across = lax.ppermute(own, "depth", SWAP)
    own_pieces, across_pieces = [own], [across]
    shift = z_shift(n_col)
    half = n_col // 2
    for step in range(1, half + 1):
        own_pieces.append(lax.ppermute(own_pieces[-1], ("col", "depth"), shift))
        if step < half:
            across_pieces.append(lax.ppermute(across_pieces[-1], ("col", "depth"), shift))
    block = jnp.stack([up] + [lax.ppermute(up, ("row", "depth"), xy_shift(s, 0)) for s in range(1, SIDE)])
    ups = [block] + [lax.ppermute(block, ("row", "depth"), xy_shift(s, 1)) for s in range(1, SIDE)]
    other = lax.ppermute(info, "depth", SWAP)

    early = lambda pieces: [pltpu.with_memory_space_constraint(x, pltpu.HBM) for x in pieces[:7]] + pieces[7:]
    own_held, across_held = early(own_pieces), early(across_pieces)
    f32 = jnp.float32
    smem, hbm, vmem = pltpu.SMEM, pltpu.HBM, pltpu.VMEM
    slots = 2 * KD
    dma = pltpu.SemaphoreType.DMA
    choice = jax.ShapeDtypeStruct((KD, *pair), f32)
    up_choice = local_kernel(up_choice_kernel, [smem] + [hbm] * SIDE, choice, hbm, [dma((KD,))])
    up_in = lax.ppermute(up_choice(info, *ups), "depth", SWAP)
    choice = jax.ShapeDtypeStruct((slots, *pair), f32)
    left_choice = local_kernel(left_choice_kernel, [smem] * 2 + [hbm] * 14, choice, hbm, [dma((slots,))])
    left_in = lax.ppermute(left_choice(info, other, *own_held[1:8], *across_held[1:8]), "depth", SWAP)
    last_in = lax.ppermute(own_pieces[8], "depth", SWAP)

    flat = pair[1:]
    tile, stack = jax.ShapeDtypeStruct(flat, f32), jax.ShapeDtypeStruct((slots, *flat), f32)
    square = jax.ShapeDtypeStruct((flat[0], slots * flat[0]), f32)
    scratch = [vmem(flat, f32), dma((slots, 2)), dma]
    up_part = local_kernel(up_kernel, [smem] + [hbm] * (SIDE + 2), (stack, stack, square), vmem, scratch, 6)
    up_sides = up_part(info, *ups, up_in, test)
    scratch = [vmem(stack.shape, f32)] * 2 + [dma((slots, 2))]
    whole = local_kernel(tile_kernel, [smem] * 2 + [hbm] * 19 + [vmem] * 3, (tile, tile), vmem, scratch, 12)
    basis, weights = whole(info, other, *own_held, *across_held, left_in, last_in, *up_sides)
    return basis[None, None, None], weights[None, None, None]


def solution(mesh):
    return jax.shard_map(
        pieces_and_tile,
        mesh=mesh,
        in_specs=(
            P("row", "depth", "col", None, None, None),
            P("row", "depth", None),
            P("col", "depth", "row", None, None, None),
            P("col", "depth", None),
            P("row", "col", None),
            P("row", "col", None, None, None),
        ),
        out_specs=(P("row", "col", "depth", None, None), P("row", "col", "depth", None, None)),
        check_vma=False,
    )
```

```python
import math

import jax
import jax.numpy as jnp
from jax import lax
from jax.experimental import pallas as pl
from jax.experimental.pallas import tpu as pltpu
from jax.sharding import PartitionSpec as P


KD = 2
CB = 8
SIDE = 4
UP_AT, TARGET_AT, ROW_AT, COL_AT, DEPTH_AT = 16, 32, 34, 35, 36


def z_shift(n_col, crossing=0):
    return [(c * 2 + (d ^ crossing), ((c + (1 - 2 * d)) % n_col) * 2 + d) for c in range(n_col) for d in (0, 1)]


def xy_shift(step, phase):
    pairs = []
    for r in range(SIDE * SIDE):
        y, x = divmod(r, SIDE)
        for d in (0, 1):
            if (d + phase) % 2 == 0:
                to = y * SIDE + (x + step) % SIDE
            else:
                to = (y + step) % SIDE * SIDE + x
            pairs.append((r * 2 + d, to * 2 + d))
    return pairs


SWAP = [(0, 1), (1, 0)]


def ring_steps(info, position):
    way = info[COL_AT] - position
    return jnp.where(info[DEPTH_AT] == 0, way, -way) & 15


def up_place(info, position):
    row = info[ROW_AT]
    dy = (row // SIDE - position // SIDE) & (SIDE - 1)
    dx = (row - position) & (SIDE - 1)
    first = info[DEPTH_AT] == 0
    return jnp.where(first, dy, dx), jnp.where(first, dx, dy)


def up_choice_kernel(info, u0, u1, u2, u3, out, sems):
    ups = (u0, u1, u2, u3)
    tile = info[TARGET_AT + 1 - info[DEPTH_AT]]
    j = tile % CB
    for k in range(KD):
        t, s = up_place(info, info[UP_AT + j * KD + k])
        for i in range(SIDE):

            @pl.when(t == i)
            def _():
                pltpu.make_async_copy(ups[i].at[s], out.at[k], sems.at[k]).start()

    for k in range(KD):
        pltpu.make_async_copy(u0.at[0], out.at[k], sems.at[k]).wait()


def left_choice_kernel(info, other, *refs):
    own, across, out, sems = refs[:8], refs[8:15], refs[15], refs[16]
    tile = info[TARGET_AT + 1 - info[DEPTH_AT]]
    b = tile // CB
    for kind, (table, pieces) in enumerate(((info, own), (other, across))):
        for k in range(KD):
            slot = (1 - kind) * KD + k
            s = ring_steps(info, table[b * KD + k])
            for i, piece in enumerate(pieces):

                @pl.when(s == i + kind)
                def _():
                    pltpu.make_async_copy(piece, out.at[slot], sems.at[slot]).start()

    for kind, (table, pieces) in enumerate(((info, own), (other, across))):
        for k in range(KD):
            slot = (1 - kind) * KD + k
            s = ring_steps(info, table[b * KD + k])

            @pl.when((s >= kind) & (s <= 7))
            def _():
                pltpu.make_async_copy(pieces[0], out.at[slot], sems.at[slot]).wait()


def parts(x):
    high = x.astype(jnp.bfloat16)
    return high, (x - high.astype(jnp.float32)).astype(jnp.bfloat16)


def dot(a, b, contract):
    dims = ((contract[:1], contract[1:]), ((), ()))
    one = lambda u, v: lax.dot_general(u, v, dims, preferred_element_type=jnp.float32)
    (a_high, a_low), (b_high, b_low) = parts(a), parts(b)
    return one(a_high, b_high) + (one(a_high, b_low) + one(a_low, b_high))


def inverse_factor(gram):
    n = gram.shape[0]
    row_id = lax.broadcasted_iota(jnp.int32, (n, n), 0)
    lane_id = lax.broadcasted_iota(jnp.int32, (n, n), 1)
    eye = jnp.where(row_id == lane_id, jnp.float32(1), jnp.float32(0))
    work = jnp.concatenate([gram, eye], axis=1)
    tall, wide = 8, 2 * n
    blocks = [work[tall * i : tall * i + tall] for i in range(n // tall)]
    sub = lax.broadcasted_iota(jnp.int32, (tall, wide), 0)
    spread = lambda x: jnp.broadcast_to(x, (tall, wide))
    for at in range(n // tall):
        below = n // tall - at
        columns = [[spread(blocks[at + i][:, tall * at + j : tall * at + j + 1]) for i in range(below)] for j in range(tall)]
        rows, scales, block = [], [], blocks[at]
        for w in range(tall):
            scale = lax.rsqrt(spread(columns[w][0][w : w + 1]))
            inverse = scale * scale
            row = spread(block[w : w + 1]) * inverse
            block = jnp.where(sub > w, block - columns[w][0] * row, block)
            rows.append(row)
            scales.append(scale)
            for j in range(w + 1, tall):
                part = spread(columns[j][0][w : w + 1]) * inverse
                for i in range(below):
                    new = columns[j][i] - columns[w][i] * part
                    columns[j][i] = new if i else jnp.where(sub > w, new, columns[j][i])
        scale = scales[-1]
        for w in range(tall - 1):
            scale = jnp.where(sub == w, scales[w], scale)
        blocks[at] = block * scale
        for i in range(1, below):
            for w in range(tall):
                blocks[at + i] = blocks[at + i] - columns[w][i] * rows[w]
    return jnp.concatenate(blocks, axis=0)[:, n:]


def up_kernel(info, u0, u1, u2, u3, up_in, sketch, ps, qs, tested, ws, up_sems, sketch_sem):
    ups = (u0, u1, u2, u3)
    depth = info[DEPTH_AT]
    j = info[TARGET_AT + depth] % CB
    n, size = ws.shape
    slots = 2 * KD

    def copies(source, slot):
        return (
            pltpu.make_async_copy(source.at[0], ps.at[slot], up_sems.at[slot, 0]),
            pltpu.make_async_copy(source.at[1], qs.at[slot], up_sems.at[slot, 1]),
        )

    pltpu.make_async_copy(sketch.at[depth], ws, sketch_sem).start()
    for k in range(KD):
        t, s = up_place(info, info[UP_AT + j * KD + k])
        for i in range(SIDE):

            @pl.when(t == i)
            def _():
                for copy in copies(ups[i].at[s], k):
                    copy.start()

        for copy in copies(up_in.at[k], KD + k):
            copy.start()
    pltpu.make_async_copy(sketch.at[0], ws, sketch_sem).wait()
    for slot in range(slots):
        for copy in copies(up_in.at[0], slot):
            copy.wait()
    tested[...] = dot(ws[...], qs[...].reshape(slots * n, size), (1, 1))


def tile_kernel(info, other, *refs):
    own, across = refs[:9], refs[9:16]
    left_in, last_in, ps, qs, tested = refs[16:21]
    basis_out, weights_out = refs[21:23]
    xs, ys, left_sems = refs[23:]
    b = info[TARGET_AT + info[DEPTH_AT]] // CB
    slots, n, size = xs.shape

    def copies(source, slot):
        return (
            pltpu.make_async_copy(source.at[1], ys.at[slot], left_sems.at[slot, 1]),
            pltpu.make_async_copy(source.at[0], xs.at[slot], left_sems.at[slot, 0]),
        )

    def start(condition, source, slot):
        @pl.when(condition)
        def _():
            for copy in copies(source, slot):
                copy.start()

    for kind, (table, pieces) in enumerate(((info, own), (other, across))):
        for k in range(KD):
            slot = kind * KD + k
            s = ring_steps(info, table[b * KD + k])
            for i, piece in enumerate(pieces):
                start(s == i + kind, piece, slot)
            if kind == 1:
                start(s == 8, last_in, slot)
            start((s > 8) | (s < kind), left_in.at[slot], slot)
    for slot in range(slots):
        for copy in copies(own[0], slot):
            copy.wait()
    middles = [dot(ys[i], ps[i], (1, 1)) for i in range(slots)]
    folded = [dot(tested[:, i * n : i * n + n], middles[i], (1, 1)) for i in range(slots)]
    sample = dot(jnp.concatenate(folded, axis=1), xs[...].reshape(slots * n, size), (1, 0))
    inverse = inverse_factor(dot(sample, sample, (1, 1)))
    turned = jnp.concatenate([dot(dot(sample, xs[i], (1, 1)), middles[i], (1, 0)) for i in range(slots)], axis=1)
    root = math.sqrt(size)
    basis_out[...] = dot(inverse * root, sample, (1, 0))
    wide = size // 4
    for at in range(0, size, wide):
        project = dot(turned, qs[:, :, at : at + wide].reshape(slots * n, wide), (1, 0))
        weights_out[:, at : at + wide] = dot(inverse * (1 / root), project, (1, 0))


def local_kernel(kernel, in_spaces, out_shape, out_space, scratch, mebibytes=1):
    return pl.pallas_call(
        kernel,
        out_shape=out_shape,
        in_specs=[pl.BlockSpec(memory_space=space) for space in in_spaces],
        out_specs=jax.tree.map(lambda _: pl.BlockSpec(memory_space=out_space), out_shape),
        scratch_shapes=scratch,
        compiler_params=pltpu.CompilerParams(vmem_limit_bytes=mebibytes << 20),
    )


def pieces_and_tile(left_store, left_home, up_store, up_home, targets, sketch):
    n_col = lax.axis_size("col")
    own, up, test = left_store[0, 0, 0], up_store[0, 0, 0], sketch[0, 0]
    pair = own.shape
    places = jnp.stack([lax.axis_index(a).astype(jnp.int32) for a in ("row", "col", "depth")])
    info = jnp.concatenate([left_home[0, 0], up_home[0, 0], targets[0, 0], places])
    axes, shift, half = ("col", "depth"), z_shift(n_col), n_col // 2
    own_pieces, across_pieces = [own], [lax.ppermute(own, axes, z_shift(n_col, 1))]
    for step in range(1, half + 1):
        own_pieces.append(lax.ppermute(own_pieces[-1], axes, shift))
        if 1 < step < half:
            across_pieces.append(lax.ppermute(across_pieces[-1], axes, shift))
    block = jnp.stack([up] + [lax.ppermute(up, ("row", "depth"), xy_shift(s, 0)) for s in range(1, SIDE)])
    ups = [block] + [lax.ppermute(block, ("row", "depth"), xy_shift(s, 1)) for s in range(1, SIDE)]
    other = lax.ppermute(info, "depth", SWAP)

    early = lambda pieces, n: [pltpu.with_memory_space_constraint(x, pltpu.HBM) for x in pieces[:n]] + pieces[n:]
    own_held, across_held = early(own_pieces, 7), early(across_pieces, 6)
    f32 = jnp.float32
    smem, hbm, vmem = pltpu.SMEM, pltpu.HBM, pltpu.VMEM
    slots = 2 * KD
    dma = pltpu.SemaphoreType.DMA
    choice = jax.ShapeDtypeStruct((KD, *pair), f32)
    up_choice = local_kernel(up_choice_kernel, [smem] + [hbm] * SIDE, choice, hbm, [dma((KD,))])
    up_in = lax.ppermute(up_choice(info, *ups), "depth", SWAP)
    choice = jax.ShapeDtypeStruct((slots, *pair), f32)
    left_choice = local_kernel(left_choice_kernel, [smem] * 2 + [hbm] * 15, choice, hbm, [dma((slots,))])
    left_in = lax.ppermute(left_choice(info, other, *own_held[:8], *across_held), "depth", SWAP)
    last_in = lax.ppermute(own_pieces[8], "depth", SWAP)

    flat = pair[1:]
    tile, stack = jax.ShapeDtypeStruct(flat, f32), jax.ShapeDtypeStruct((slots, *flat), f32)
    square = jax.ShapeDtypeStruct((flat[0], slots * flat[0]), f32)
    scratch = [vmem(flat, f32), dma((slots, 2)), dma]
    up_part = local_kernel(up_kernel, [smem] + [hbm] * (SIDE + 2), (stack, stack, square), vmem, scratch, 6)
    up_sides = up_part(info, *ups, up_in, test)
    scratch = [vmem(stack.shape, f32)] * 2 + [dma((slots, 2))]
    whole = local_kernel(tile_kernel, [smem] * 2 + [hbm] * 18 + [vmem] * 3, (tile, tile), vmem, scratch, 12)
    basis, weights = whole(info, other, *own_held, *across_held, left_in, last_in, *up_sides)
    return basis[None, None, None], weights[None, None, None]


def solution(mesh):
    return jax.shard_map(
        pieces_and_tile,
        mesh=mesh,
        in_specs=(
            P("row", "depth", "col", None, None, None),
            P("row", "depth", None),
            P("col", "depth", "row", None, None, None),
            P("col", "depth", None),
            P("row", "col", None),
            P("row", "col", None, None, None),
        ),
        out_specs=(P("row", "col", "depth", None, None), P("row", "col", "depth", None, None)),
        check_vma=False,
    )
```

```python
import math

import jax
import jax.numpy as jnp
from jax import lax
from jax.experimental import pallas as pl
from jax.experimental.pallas import tpu as pltpu
from jax.sharding import PartitionSpec as P


KD = 2
CB = 8
SIDE = 4
UP_AT, TARGET_AT, ROW_AT, COL_AT, DEPTH_AT = 16, 32, 34, 35, 36


def z_shift(n_col, crossing=0):
    return [(c * 2 + (d ^ crossing), ((c + (1 - 2 * d)) % n_col) * 2 + d) for c in range(n_col) for d in (0, 1)]


def xy_shift(step, phase):
    pairs = []
    for r in range(SIDE * SIDE):
        y, x = divmod(r, SIDE)
        for d in (0, 1):
            if (d + phase) % 2 == 0:
                to = y * SIDE + (x + step) % SIDE
            else:
                to = (y + step) % SIDE * SIDE + x
            pairs.append((r * 2 + d, to * 2 + d))
    return pairs


SWAP = [(0, 1), (1, 0)]


def ring_steps(info, position):
    way = info[COL_AT] - position
    return jnp.where(info[DEPTH_AT] == 0, way, -way) & 15


def up_place(info, position):
    row = info[ROW_AT]
    dy = (row // SIDE - position // SIDE) & (SIDE - 1)
    dx = (row - position) & (SIDE - 1)
    first = info[DEPTH_AT] == 0
    return jnp.where(first, dy, dx), jnp.where(first, dx, dy)


def draw(ws, ps, qs, drawn):
    n, size = ws.shape
    tested = dot(ws[...], qs[...].reshape(KD * n, size), (1, 1))
    for k in range(KD):
        drawn[k] = dot(tested[:, k * n : k * n + n], ps[k], (1, 0))


def up_kernel(info, u0, u1, u2, u3, out, ps, qs, sems, own_sems):
    ups = (u0, u1, u2, u3)
    depth = info[DEPTH_AT]
    j_own, j_other = info[TARGET_AT + depth] % CB, info[TARGET_AT + 1 - depth] % CB

    def copies(source, k):
        return (
            pltpu.make_async_copy(source.at[1], qs.at[k], own_sems.at[k, 1]),
            pltpu.make_async_copy(source.at[0], ps.at[k], own_sems.at[k, 0]),
        )

    for k in range(KD):
        t, s = up_place(info, info[UP_AT + j_other * KD + k])
        t_own, s_own = up_place(info, info[UP_AT + j_own * KD + k])
        for i in range(SIDE):

            @pl.when(t == i)
            def _():
                pltpu.make_async_copy(ups[i].at[s], out.at[k], sems.at[k]).start()

            @pl.when(t_own == i)
            def _():
                for copy in copies(ups[i].at[s_own], k):
                    copy.start()

    for k in range(KD):
        for copy in copies(u0.at[0], k):
            copy.wait()
    for k in range(KD):
        pltpu.make_async_copy(u0.at[0], out.at[k], sems.at[k]).wait()


def left_choice_kernel(info, other, *refs):
    own, across, out, sems = refs[:8], refs[8:15], refs[15], refs[16]
    tile = info[TARGET_AT + 1 - info[DEPTH_AT]]
    b = tile // CB
    for kind, (table, pieces) in enumerate(((info, own), (other, across))):
        for k in range(KD):
            slot = (1 - kind) * KD + k
            s = ring_steps(info, table[b * KD + k])
            for i, piece in enumerate(pieces):

                @pl.when(s == i + kind)
                def _():
                    pltpu.make_async_copy(piece, out.at[slot], sems.at[slot]).start()

    for kind, (table, pieces) in enumerate(((info, own), (other, across))):
        for k in range(KD):
            slot = (1 - kind) * KD + k
            s = ring_steps(info, table[b * KD + k])

            @pl.when((s >= kind) & (s <= 7))
            def _():
                pltpu.make_async_copy(pieces[0], out.at[slot], sems.at[slot]).wait()


def parts(x):
    high = x.astype(jnp.bfloat16)
    return high, (x - high.astype(jnp.float32)).astype(jnp.bfloat16)


def dot(a, b, contract):
    dims = ((contract[:1], contract[1:]), ((), ()))
    one = lambda u, v: lax.dot_general(u, v, dims, preferred_element_type=jnp.float32)
    (a_high, a_low), (b_high, b_low) = parts(a), parts(b)
    return one(a_high, b_high) + (one(a_high, b_low) + one(a_low, b_high))


def inverse_factor(gram):
    n = gram.shape[0]
    row_id = lax.broadcasted_iota(jnp.int32, (n, n), 0)
    lane_id = lax.broadcasted_iota(jnp.int32, (n, n), 1)
    eye = jnp.where(row_id == lane_id, jnp.float32(1), jnp.float32(0))
    work = jnp.concatenate([gram, eye], axis=1)
    tall, wide = 8, 2 * n
    blocks = [work[tall * i : tall * i + tall] for i in range(n // tall)]
    sub = lax.broadcasted_iota(jnp.int32, (tall, wide), 0)
    spread = lambda x: jnp.broadcast_to(x, (tall, wide))
    for at in range(n // tall):
        below = n // tall - at
        columns = [[spread(blocks[at + i][:, tall * at + j : tall * at + j + 1]) for i in range(below)] for j in range(tall)]
        block, rows, steps = blocks[at], [], []
        for w in range(0, tall, 2):
            first, second = columns[w], columns[w + 1]
            a, b, c = spread(first[0][w : w + 1]), spread(first[0][w + 1 : w + 2]), spread(second[0][w + 1 : w + 2])
            det_root = lax.rsqrt(a * c - b * b)
            scale = det_root * det_root
            ia, ib, ic = c * scale, -b * scale, a * scale
            for j in range(w + 2, tall):
                p, q = spread(columns[j][0][w : w + 1]), spread(columns[j][0][w + 1 : w + 2])
                s, t = ia * p + ib * q, ib * p + ic * q
                columns[j] = [columns[j][i] - first[i] * s - second[i] * t for i in range(below)]
            p, q = spread(block[w : w + 1]), spread(block[w + 1 : w + 2])
            s, t = ia * p + ib * q, ib * p + ic * q
            if w + 2 < tall:
                block = block - first[0] * s - second[0] * t
            steps.append((first, second, s, t))
            a_root = lax.rsqrt(a)
            rows += [p * a_root, (q - b * (a_root * a_root) * p) * (det_root * (a * a_root))]
        done = rows[-1]
        for w in range(tall - 1):
            done = jnp.where(sub == w, rows[w], done)
        blocks[at] = done
        for i in range(1, below):
            for first, second, s, t in steps:
                blocks[at + i] = blocks[at + i] - first[i] * s - second[i] * t
    return jnp.concatenate(blocks, axis=0)[:, n:]


def across_kernel(info, up_in, sketch, ps_own, qs_own, ps, qs, drawn_own, drawn, ws, sems, sketch_sem):
    sketch_copy = pltpu.make_async_copy(sketch.at[info[DEPTH_AT]], ws, sketch_sem)
    copies = [pltpu.make_async_copy(up_in.at[k, 1 - i], (qs, ps)[i].at[k], sems.at[k, i]) for k in range(KD) for i in range(2)]
    for copy in (sketch_copy, *copies):
        copy.start()
    sketch_copy.wait()
    draw(ws, ps_own, qs_own, drawn_own)
    for copy in copies:
        copy.wait()
    draw(ws, ps, qs, drawn)


def tile_kernel(info, other, *refs):
    own, across = refs[:9], refs[9:16]
    left_in, last_in = refs[16:18]
    ps, qs, drawn = refs[18:24:3], refs[19:24:3], refs[20:24:3]
    basis_out, weights_out, pairs, basis, weights, left_sems, out_sems = refs[24:]
    b = info[TARGET_AT + info[DEPTH_AT]] // CB
    slots, _, n, size = pairs.shape

    def start(condition, source, slot):
        @pl.when(condition)
        def _():
            pltpu.make_async_copy(source, pairs.at[slot], left_sems.at[slot]).start()

    for kind, (table, pieces) in enumerate(((info, own), (other, across))):
        for k in range(KD):
            slot = kind * KD + k
            s = ring_steps(info, table[b * KD + k])
            for i, piece in enumerate(pieces):
                start(s == i + kind, piece, slot)
            if kind == 1:
                start(s == 8, last_in, slot)
            start((s > 8) | (s < kind), left_in.at[slot], slot)
    for slot in range(slots):
        pltpu.make_async_copy(own[0], pairs.at[slot], left_sems.at[slot]).wait()
    folded = [dot(drawn[i // KD][i % KD], pairs[i, 1], (1, 1)) for i in range(slots)]
    x_all = jnp.concatenate([pairs[i, 0] for i in range(slots)], axis=0)
    sample = dot(jnp.concatenate(folded, axis=1), x_all, (1, 0))
    inverse = inverse_factor(dot(sample, sample, (1, 1)))
    middles = [dot(pairs[i, 1], ps[i // KD][i % KD], (1, 1)) for i in range(slots)]
    turned = [dot(dot(sample, pairs[i, 0], (1, 1)), middles[i], (1, 0)) for i in range(slots)]
    turned = [jnp.concatenate(turned[i : i + KD], axis=1) for i in (0, KD)]
    root = math.sqrt(size)
    basis[...] = dot(inverse * root, sample, (1, 0))
    done = [pltpu.make_async_copy(basis, basis_out, out_sems.at[0])]
    done[0].start()
    wide = size // 4
    for i in range(4):
        at = slice(i * wide, i * wide + wide)
        project = sum(dot(t, q[:, :, at].reshape(KD * n, wide), (1, 0)) for t, q in zip(turned, qs))
        weights[:, at] = dot(inverse * (1 / root), project, (1, 0))
        done.append(pltpu.make_async_copy(weights.at[:, at], weights_out.at[:, at], out_sems.at[i + 1]))
        done[-1].start()
    for copy in done:
        copy.wait()


def local_kernel(kernel, in_spaces, out_shape, out_spaces, scratch, mebibytes=1):
    return pl.pallas_call(
        kernel,
        out_shape=out_shape,
        in_specs=[pl.BlockSpec(memory_space=space) for space in in_spaces],
        out_specs=tuple(pl.BlockSpec(memory_space=space) for space in out_spaces),
        scratch_shapes=scratch,
        compiler_params=pltpu.CompilerParams(vmem_limit_bytes=mebibytes << 20),
    )


def pieces_and_tile(left_store, left_home, up_store, up_home, targets, sketch):
    n_col = lax.axis_size("col")
    own, up, test = left_store[0, 0, 0], up_store[0, 0, 0], sketch[0, 0]
    pair = own.shape
    places = jnp.stack([lax.axis_index(a).astype(jnp.int32) for a in ("row", "col", "depth")])
    info = jnp.concatenate([left_home[0, 0], up_home[0, 0], targets[0, 0], places])
    axes, shift, half = ("col", "depth"), z_shift(n_col), n_col // 2
    own_pieces, across_pieces = [own], [lax.ppermute(own, axes, z_shift(n_col, 1))]
    for step in range(1, half + 1):
        own_pieces.append(lax.ppermute(own_pieces[-1], axes, shift))
        if 1 < step < half:
            across_pieces.append(lax.ppermute(across_pieces[-1], axes, shift))
    block = jnp.stack([up] + [lax.ppermute(up, ("row", "depth"), xy_shift(s, 0)) for s in range(1, SIDE)])
    ups = [block] + [lax.ppermute(block, ("row", "depth"), xy_shift(s, 1)) for s in range(1, SIDE)]
    other = lax.ppermute(info, "depth", SWAP)

    early = lambda pieces, n: [pltpu.with_memory_space_constraint(x, pltpu.HBM) for x in pieces[:n]] + pieces[n:]
    own_held, across_held = early(own_pieces, 7), early(across_pieces, 6)
    f32 = jnp.float32
    smem, hbm, vmem = pltpu.SMEM, pltpu.HBM, pltpu.VMEM
    slots = 2 * KD
    dma = pltpu.SemaphoreType.DMA
    flat = pair[1:]
    array = lambda *shape: jax.ShapeDtypeStruct(shape, f32)
    tile, couple = array(*flat), array(KD, *flat)
    tile_scratch = vmem(flat, f32)

    outs = array(KD, *pair), couple, couple
    scratch = [dma((KD,)), dma((KD, 2))]
    up_part = local_kernel(up_kernel, [smem] + [hbm] * SIDE, outs, [hbm] + [vmem] * 2, scratch, 6)
    choice, p_own, q_own = up_part(info, *ups)
    up_in = lax.ppermute(choice, "depth", SWAP)
    left_choice = local_kernel(left_choice_kernel, [smem] * 2 + [hbm] * 15, (array(slots, *pair),), [hbm], [dma((slots,))])
    left_in = lax.ppermute(left_choice(info, other, *own_held[:8], *across_held)[0], "depth", SWAP)
    last_in = lax.ppermute(own_pieces[8], "depth", SWAP)

    scratch = [tile_scratch, dma((KD, 2)), dma]
    across_part = local_kernel(across_kernel, [smem] + [hbm] * 2 + [vmem] * 2, (couple,) * 4, [vmem] * 4, scratch, 6)
    p_across, q_across, drawn_own, drawn_across = across_part(info, up_in, test, p_own, q_own)
    sides = p_own, q_own, drawn_own, p_across, q_across, drawn_across
    scratch = [vmem((slots, *pair), f32)] + [tile_scratch] * 2 + [dma((slots,)), dma((5,))]
    whole = local_kernel(tile_kernel, [smem] * 2 + [hbm] * 18 + [vmem] * 6, (tile, tile), [hbm] * 2, scratch, 12)
    basis, weights = whole(info, other, *own_held, *across_held, left_in, last_in, *sides)
    return basis[None, None, None], weights[None, None, None]


def solution(mesh):
    return jax.shard_map(
        pieces_and_tile,
        mesh=mesh,
        in_specs=(
            P("row", "depth", "col", None, None, None),
            P("row", "depth", None),
            P("col", "depth", "row", None, None, None),
            P("col", "depth", None),
            P("row", "col", None),
            P("row", "col", None, None, None),
        ),
        out_specs=(P("row", "col", "depth", None, None), P("row", "col", "depth", None, None)),
        check_vma=False,
    )
```

```python
import math

import jax
import jax.numpy as jnp
from jax import lax
from jax.experimental import pallas as pl
from jax.experimental.pallas import tpu as pltpu
from jax.sharding import PartitionSpec as P


KD = 2
CB = 8
SIDE = 4
UP_AT, TARGET_AT, ROW_AT, COL_AT, DEPTH_AT = 16, 32, 34, 35, 36


def z_shift(n_col, crossing=0):
    return [(c * 2 + (d ^ crossing), ((c + (1 - 2 * d)) % n_col) * 2 + d) for c in range(n_col) for d in (0, 1)]


def xy_shift(step, phase):
    pairs = []
    for r in range(SIDE * SIDE):
        y, x = divmod(r, SIDE)
        for d in (0, 1):
            if (d + phase) % 2 == 0:
                to = y * SIDE + (x + step) % SIDE
            else:
                to = (y + step) % SIDE * SIDE + x
            pairs.append((r * 2 + d, to * 2 + d))
    return pairs


SWAP = [(0, 1), (1, 0)]


def ring_steps(info, position):
    way = info[COL_AT] - position
    return jnp.where(info[DEPTH_AT] == 0, way, -way) & 15


def up_place(info, position):
    row = info[ROW_AT]
    dy = (row // SIDE - position // SIDE) & (SIDE - 1)
    dx = (row - position) & (SIDE - 1)
    first = info[DEPTH_AT] == 0
    return jnp.where(first, dy, dx), jnp.where(first, dx, dy)


def draw(ws, ps, qs, drawn):
    n, size = ws.shape
    tested = dot(ws[...], qs[...].reshape(KD * n, size), (1, 1))
    for k in range(KD):
        drawn[k] = dot(tested[:, k * n : k * n + n], ps[k], (1, 0))


def up_kernel(info, u0, u1, u2, u3, sketch, out, ps, qs, drawn, ws, sems, own_sems, sketch_sem):
    ups = (u0, u1, u2, u3)
    depth = info[DEPTH_AT]
    j_own, j_other = info[TARGET_AT + depth] % CB, info[TARGET_AT + 1 - depth] % CB

    def copies(source, k):
        return (
            pltpu.make_async_copy(source.at[1], qs.at[k], own_sems.at[k, 1]),
            pltpu.make_async_copy(source.at[0], ps.at[k], own_sems.at[k, 0]),
        )

    pltpu.make_async_copy(sketch.at[depth], ws, sketch_sem).start()
    for k in range(KD):
        t, s = up_place(info, info[UP_AT + j_other * KD + k])
        t_own, s_own = up_place(info, info[UP_AT + j_own * KD + k])
        for i in range(SIDE):

            @pl.when(t == i)
            def _():
                pltpu.make_async_copy(ups[i].at[s], out.at[k], sems.at[k]).start()

            @pl.when(t_own == i)
            def _():
                for copy in copies(ups[i].at[s_own], k):
                    copy.start()

    pltpu.make_async_copy(sketch.at[0], ws, sketch_sem).wait()
    for k in range(KD):
        for copy in copies(u0.at[0], k):
            copy.wait()
    draw(ws, ps, qs, drawn)
    for k in range(KD):
        pltpu.make_async_copy(u0.at[0], out.at[k], sems.at[k]).wait()


def left_choice_kernel(info, other, *refs):
    own, across, out, sems = refs[:8], refs[8:15], refs[15], refs[16]
    tile = info[TARGET_AT + 1 - info[DEPTH_AT]]
    b = tile // CB
    for kind, (table, pieces) in enumerate(((info, own), (other, across))):
        for k in range(KD):
            slot = (1 - kind) * KD + k
            s = ring_steps(info, table[b * KD + k])
            for i, piece in enumerate(pieces):

                @pl.when(s == i + kind)
                def _():
                    pltpu.make_async_copy(piece, out.at[slot], sems.at[slot]).start()

    for kind, (table, pieces) in enumerate(((info, own), (other, across))):
        for k in range(KD):
            slot = (1 - kind) * KD + k
            s = ring_steps(info, table[b * KD + k])

            @pl.when((s >= kind) & (s <= 7))
            def _():
                pltpu.make_async_copy(pieces[0], out.at[slot], sems.at[slot]).wait()


def parts(x):
    high = x.astype(jnp.bfloat16)
    return high, (x - high.astype(jnp.float32)).astype(jnp.bfloat16)


def dot(a, b, contract):
    dims = ((contract[:1], contract[1:]), ((), ()))
    one = lambda u, v: lax.dot_general(u, v, dims, preferred_element_type=jnp.float32)
    (a_high, a_low), (b_high, b_low) = parts(a), parts(b)
    return one(a_high, b_high) + (one(a_high, b_low) + one(a_low, b_high))


def inverse_factor(gram):
    n = gram.shape[0]
    row_id = lax.broadcasted_iota(jnp.int32, (n, n), 0)
    lane_id = lax.broadcasted_iota(jnp.int32, (n, n), 1)
    eye = jnp.where(row_id == lane_id, jnp.float32(1), jnp.float32(0))
    work = jnp.concatenate([gram, eye], axis=1)
    tall, wide = 8, 2 * n
    blocks = [work[tall * i : tall * i + tall] for i in range(n // tall)]
    sub = lax.broadcasted_iota(jnp.int32, (tall, wide), 0)
    spread = lambda x: jnp.broadcast_to(x, (tall, wide))
    for at in range(n // tall):
        below = n // tall - at
        columns = [[spread(blocks[at + i][:, tall * at + j : tall * at + j + 1]) for i in range(below)] for j in range(tall)]
        block, rows, steps = blocks[at], [], []
        for w in range(0, tall, 2):
            first, second = columns[w], columns[w + 1]
            a, b, c = spread(first[0][w : w + 1]), spread(first[0][w + 1 : w + 2]), spread(second[0][w + 1 : w + 2])
            det_root = lax.rsqrt(a * c - b * b)
            scale = det_root * det_root
            ia, ib, ic = c * scale, -b * scale, a * scale
            for j in range(w + 2, tall):
                p, q = spread(columns[j][0][w : w + 1]), spread(columns[j][0][w + 1 : w + 2])
                s, t = ia * p + ib * q, ib * p + ic * q
                columns[j] = [columns[j][i] - first[i] * s - second[i] * t for i in range(below)]
            p, q = spread(block[w : w + 1]), spread(block[w + 1 : w + 2])
            s, t = ia * p + ib * q, ib * p + ic * q
            if w + 2 < tall:
                block = block - first[0] * s - second[0] * t
            steps.append((first, second, s, t))
            a_root = lax.rsqrt(a)
            rows += [p * a_root, (q - b * (a_root * a_root) * p) * (det_root * (a * a_root))]
        done = rows[-1]
        for w in range(tall - 1):
            done = jnp.where(sub == w, rows[w], done)
        blocks[at] = done
        for i in range(1, below):
            for first, second, s, t in steps:
                blocks[at + i] = blocks[at + i] - first[i] * s - second[i] * t
    return jnp.concatenate(blocks, axis=0)[:, n:]


def across_kernel(info, up_in, sketch, ps, qs, drawn, ws, sems, sketch_sem):
    sketch_copy = pltpu.make_async_copy(sketch.at[info[DEPTH_AT]], ws, sketch_sem)
    copies = [pltpu.make_async_copy(up_in.at[k, 1 - i], (qs, ps)[i].at[k], sems.at[k, i]) for k in range(KD) for i in range(2)]
    for copy in (sketch_copy, *copies):
        copy.start()
    for copy in (sketch_copy, *copies):
        copy.wait()
    draw(ws, ps, qs, drawn)


def tile_kernel(info, other, *refs):
    own, across = refs[:9], refs[9:16]
    left_in, last_in = refs[16:18]
    ps, qs, drawn = refs[18:24:3], refs[19:24:3], refs[20:24:3]
    basis_out, weights_out, pairs, basis, weights, left_sems, out_sems = refs[24:]
    b = info[TARGET_AT + info[DEPTH_AT]] // CB
    slots, _, n, size = pairs.shape

    def start(condition, source, slot):
        @pl.when(condition)
        def _():
            pltpu.make_async_copy(source, pairs.at[slot], left_sems.at[slot]).start()

    for kind, (table, pieces) in enumerate(((info, own), (other, across))):
        for k in range(KD):
            slot = kind * KD + k
            s = ring_steps(info, table[b * KD + k])
            for i, piece in enumerate(pieces):
                start(s == i + kind, piece, slot)
            if kind == 1:
                start(s == 8, last_in, slot)
            start((s > 8) | (s < kind), left_in.at[slot], slot)
    for slot in range(slots):
        pltpu.make_async_copy(own[0], pairs.at[slot], left_sems.at[slot]).wait()
    folded = [dot(drawn[i // KD][i % KD], pairs[i, 1], (1, 1)) for i in range(slots)]
    x_all = jnp.concatenate([pairs[i, 0] for i in range(slots)], axis=0)
    sample = dot(jnp.concatenate(folded, axis=1), x_all, (1, 0))
    inverse = inverse_factor(dot(sample, sample, (1, 1)))
    middles = [dot(pairs[i, 1], ps[i // KD][i % KD], (1, 1)) for i in range(slots)]
    turned = [dot(dot(sample, pairs[i, 0], (1, 1)), middles[i], (1, 0)) for i in range(slots)]
    turned = [jnp.concatenate(turned[i : i + KD], axis=1) for i in (0, KD)]
    root = math.sqrt(size)
    basis[...] = dot(inverse * root, sample, (1, 0))
    done = [pltpu.make_async_copy(basis, basis_out, out_sems.at[0])]
    done[0].start()
    wide = size // 4
    for i in range(4):
        at = slice(i * wide, i * wide + wide)
        project = sum(dot(t, q[:, :, at].reshape(KD * n, wide), (1, 0)) for t, q in zip(turned, qs))
        weights[:, at] = dot(inverse * (1 / root), project, (1, 0))
        done.append(pltpu.make_async_copy(weights.at[:, at], weights_out.at[:, at], out_sems.at[i + 1]))
        done[-1].start()
    for copy in done:
        copy.wait()


def local_kernel(kernel, in_spaces, out_shape, out_spaces, scratch, mebibytes=1):
    return pl.pallas_call(
        kernel,
        out_shape=out_shape,
        in_specs=[pl.BlockSpec(memory_space=space) for space in in_spaces],
        out_specs=tuple(pl.BlockSpec(memory_space=space) for space in out_spaces),
        scratch_shapes=scratch,
        compiler_params=pltpu.CompilerParams(vmem_limit_bytes=mebibytes << 20),
    )


def pieces_and_tile(left_store, left_home, up_store, up_home, targets, sketch):
    n_col = lax.axis_size("col")
    own, up, test = left_store[0, 0, 0], up_store[0, 0, 0], sketch[0, 0]
    pair = own.shape
    places = jnp.stack([lax.axis_index(a).astype(jnp.int32) for a in ("row", "col", "depth")])
    info = jnp.concatenate([left_home[0, 0], up_home[0, 0], targets[0, 0], places])
    axes, shift, half = ("col", "depth"), z_shift(n_col), n_col // 2
    own_pieces, across_pieces = [own], [lax.ppermute(own, axes, z_shift(n_col, 1))]
    for step in range(1, half + 1):
        own_pieces.append(lax.ppermute(own_pieces[-1], axes, shift))
        if 1 < step < half:
            across_pieces.append(lax.ppermute(across_pieces[-1], axes, shift))
    block = jnp.stack([up] + [lax.ppermute(up, ("row", "depth"), xy_shift(s, 0)) for s in range(1, SIDE)])
    ups = [block] + [lax.ppermute(block, ("row", "depth"), xy_shift(s, 1)) for s in range(1, SIDE)]
    other = lax.ppermute(info, "depth", SWAP)

    early = lambda pieces, n: [pltpu.with_memory_space_constraint(x, pltpu.HBM) for x in pieces[:n]] + pieces[n:]
    own_held, across_held = early(own_pieces, 7), early(across_pieces, 6)
    f32 = jnp.float32
    smem, hbm, vmem = pltpu.SMEM, pltpu.HBM, pltpu.VMEM
    slots = 2 * KD
    dma = pltpu.SemaphoreType.DMA
    flat = pair[1:]
    array = lambda *shape: jax.ShapeDtypeStruct(shape, f32)
    tile, couple = array(*flat), array(KD, *flat)
    tile_scratch = vmem(flat, f32)

    outs = array(KD, *pair), couple, couple, couple
    scratch = [tile_scratch, dma((KD,)), dma((KD, 2)), dma]
    up_part = local_kernel(up_kernel, [smem] + [hbm] * (SIDE + 1), outs, [hbm] + [vmem] * 3, scratch, 6)
    choice, p_own, q_own, drawn_own = up_part(info, *ups, test)
    up_in = lax.ppermute(choice, "depth", SWAP)
    left_choice = local_kernel(left_choice_kernel, [smem] * 2 + [hbm] * 15, (array(slots, *pair),), [hbm], [dma((slots,))])
    left_in = lax.ppermute(left_choice(info, other, *own_held[:8], *across_held)[0], "depth", SWAP)
    last_in = lax.ppermute(own_pieces[8], "depth", SWAP)

    scratch = [tile_scratch, dma((KD, 2)), dma]
    across_part = local_kernel(across_kernel, [smem] + [hbm] * 2, (couple, couple, couple), [vmem] * 3, scratch, 4)
    sides = p_own, q_own, drawn_own, *across_part(info, up_in, test)
    scratch = [vmem((slots, *pair), f32)] + [tile_scratch] * 2 + [dma((slots,)), dma((5,))]
    whole = local_kernel(tile_kernel, [smem] * 2 + [hbm] * 18 + [vmem] * 6, (tile, tile), [hbm] * 2, scratch, 12)
    basis, weights = whole(info, other, *own_held, *across_held, left_in, last_in, *sides)
    return basis[None, None, None], weights[None, None, None]


def solution(mesh):
    return jax.shard_map(
        pieces_and_tile,
        mesh=mesh,
        in_specs=(
            P("row", "depth", "col", None, None, None),
            P("row", "depth", None),
            P("col", "depth", "row", None, None, None),
            P("col", "depth", None),
            P("row", "col", None),
            P("row", "col", None, None, None),
        ),
        out_specs=(P("row", "col", "depth", None, None), P("row", "col", "depth", None, None)),
        check_vma=False,
    )
```
